32 devices in a mesh: row: 4 (over x, core), col: 8 (over z, y).
Axes of the slice: x: 2, y: 2, z: 4, core: 2. Of those that a mesh axis runs over, the one named last changes fastest.
Arguments:
- heat_source: bfloat16 [262144, 128], P(('row', 'col')), may hold values from -6 to 6
- diagonal: float32 [262144], P(('row', 'col')), may hold values from 3 to 8
- active: int32 [262144], P(('row', 'col')), may hold values 0 or 1
- conductance: bfloat16 [2048, 7, 128, 128], P(('row', 'col')), may hold values from -0.1875 to 0.1875
- pattern: int32 [2048, 7], P(('row', 'col')), may hold values from 0 to 127, as said below
- send_list: int32 [32, 4, 16], P(('row', 'col')), may hold values from 0 to 63
- owner_map: int32 [2, 2048], replicated, may hold values from 0 to 63, as said below
- displacement: bfloat16 [64, 32, 128, 128], P('row', 'col'), may hold values from -6 to 6
- bond_live: int32 [6, 64, 32, 128], P(None, 'row', 'col'), may hold values from 0 to 1, as said below
Outputs:
- brick_temperature: bfloat16 [64, 32, 128, 128], P('row', 'col')
- moved: bfloat16 [64, 32, 128, 128], P('row', 'col')
The draws below stay inside these ranges and needn't reach their ends.
Inputs may be any that keep to these rules, and one draw needn't show every extreme that they name: `pattern`: tile 0 of a block row reads the block itself (its row within the device); tile 1 reads received slot 64 + that row. `owner_map`: every brick slot receives exactly one block. Brick slot s is fed from the device a fixed cyclic distance back along the curve order, the same distance for every brick; one device sends exactly 2 blocks to some bricks and at most that to any. bond_live[d + 3] at a cell equals bond_live[d] at the cell one step back along direction d, and 0 where that cell lies outside the grid; bonds leaving the grid in + directions are 0. `send_list`: local block indices.
All inputs are finite; a program needn't handle non-finite values. No bound on the sum of `active` on one device may be relied on, other than what follows from the above.
Results may differ from the reference program's by a relative error of at most 0.004.
Values may be sent and summed in bfloat16 or wider, within the bound.
A program may use at most 192 MiB of HBM per device.

```python
import math
import jax
import jax.numpy as jnp
from jax import lax

BX = 16
BY = 4
NODES_PER_COLUMN = 128
PROCESS_CASES = 128
TILES = 7
ITERS = 3
BLK_DEV = 64
GHOST_CAP = 16
PATH_SEGMENTS = 2048
POINTS = 262144
X = 64
Y = 32
N_ROW = 4
N_COL = 8
DEVICES = 32


def draw_pattern(key, part):
    rows_local = jnp.arange(PATH_SEGMENTS, dtype=jnp.int32) % BLK_DEV
    others = jax.random.randint(key, (PATH_SEGMENTS, TILES - 2), 0, 2 * BLK_DEV, dtype=jnp.int32)
    return jnp.concatenate([rows_local[:, None], (rows_local + BLK_DEV)[:, None], others], 1).astype(jnp.int32)


def draw_owner_map(key, part):
    first_key, second_key = jax.random.split(jax.random.fold_in(key, 11))
    span = max(DEVICES, BLK_DEV)
    scores = jax.random.permutation(first_key, span).astype(jnp.int32)
    values = jnp.arange(span, dtype=jnp.int32)
    scores = jnp.where(values == 1, -2, scores)
    scores = jnp.where(values == DEVICES // 2, -1, scores)
    ordered = jnp.argsort(scores, stable=True).astype(jnp.int32)
    offsets = ordered[:BLK_DEV] % DEVICES
    slots = jax.vmap(lambda subkey: jax.random.permutation(subkey, BLK_DEV))(jax.random.split(second_key, DEVICES))
    sources = jnp.arange(DEVICES, dtype=jnp.int32)[:, None]
    targets = (sources + offsets[slots]) % DEVICES
    return jnp.stack([targets.reshape(-1), slots.reshape(-1)]).astype(jnp.int32)


def draw_bond_live(key, part):
    raw = jax.random.randint(key, (3, X, Y, NODES_PER_COLUMN), 0, 8, dtype=jnp.int32)
    live = (raw < 7).astype(jnp.int32)
    plus_x = live[0].at[-1].set(0)
    plus_y = live[1].at[:, -1].set(0)
    plus_z = live[2].at[:, :, -1].set(0)
    minus_x = jnp.concatenate([jnp.zeros_like(plus_x[:1]), plus_x[:-1]], 0)
    minus_y = jnp.concatenate([jnp.zeros_like(plus_y[:, :1]), plus_y[:, :-1]], 1)
    minus_z = jnp.concatenate([jnp.zeros_like(plus_z[:, :, :1]), plus_z[:, :, :-1]], 2)
    return jnp.stack([plus_x, plus_y, plus_z, minus_x, minus_y, minus_z]).astype(jnp.int32)


def touch_ends(drawn, stream_key, smallest, high):
    longest = drawn.shape.index(max(drawn.shape))
    spots = []
    for shift in (0, 1):
        where = [jax.random.randint(jax.random.fold_in(stream_key, axis), (), 0, length) for axis, length in enumerate(drawn.shape)]
        where[longest] = (where[longest] + shift) % drawn.shape[longest]
        spots.append(tuple(where))
    return drawn.at[spots[0]].set(smallest).at[spots[1]].set(high)


def levels(stream_key, dims, cuts, smallest, high):
    gain = 1.0
    for dim, shards_of in cuts:
        draws = jax.random.uniform(jax.random.fold_in(jax.random.fold_in(stream_key, 6), dim), (shards_of,), jnp.float32, smallest / len(cuts), high / len(cuts))
        gain = gain * jnp.repeat(jnp.exp(draws), dims[dim] // shards_of).reshape((-1,) + (1,) * (len(dims) - 1 - dim))
    return gain


def gaussian(key, extent, deviation, most, cuts=(), held_as=jnp.bfloat16):
    drawn = deviation * jax.random.normal(key, extent, jnp.float32)
    if cuts:
        drawn = drawn * levels(key, extent, cuts, -0.22, 0.18)
    return jnp.clip(drawn, -most, most).astype(held_as)


def setup_inputs(seed: int = 0) -> dict:
    splits = jax.random.split(jax.random.key(seed), 10)
    return {
        "heat_source": gaussian(splits[0], (POINTS, PROCESS_CASES), 1.0, 6.0, ((0, 32),)),
        "diagonal": jnp.clip(jnp.exp(math.log(8.0) - 0.98082925 * jax.random.uniform(splits[1], (POINTS,), jnp.float32) ** levels(splits[1], (POINTS,), ((0, 32),), -0.2, 0.2)), 3.0, 8.0),
        "active": touch_ends((jax.random.randint(splits[2], (POINTS,), 0, 4) < 3).astype(jnp.int32), jax.random.fold_in(splits[2], 1), 0, 1),
        "conductance": gaussian(splits[3], (PATH_SEGMENTS, TILES, NODES_PER_COLUMN, NODES_PER_COLUMN), (TILES * NODES_PER_COLUMN) ** -0.5, 0.1875, ((0, 32),)),
        "pattern": draw_pattern(jax.random.fold_in(splits[9], 71), 0),
        "send_list": touch_ends(jax.random.randint(splits[5], (DEVICES, 4, GHOST_CAP), 0, BX * BY), jax.random.fold_in(splits[5], 1), 0, (BX * BY) - 1).astype(jnp.int32),
        "owner_map": draw_owner_map(jax.random.fold_in(splits[9], 71), 0),
        "displacement": gaussian(splits[7], (X, Y, NODES_PER_COLUMN, PROCESS_CASES), 1.0, 6.0, ((0, 4), (1, 8))),
        "bond_live": draw_bond_live(jax.random.fold_in(splits[9], 71), 0),
    }


LOWER = 1.0
UPPER = 10.0
ALPHA_T = 0.5
BOND_STIFFNESS = 1.0
STATE_STIFFNESS = 2.0
STEP_SIZE = 0.1
GHOST_STEPS = (1, -1, 2, -2)


def chebyshev_weights(count):
    center = (UPPER + LOWER) / 2.0
    half_width = (UPPER - LOWER) / 2.0
    ratio_value = center / half_width
    previous = 1.0 / ratio_value
    weights = []
    for step_number in range(count):
        current = 1.0 / (2.0 * ratio_value - previous)
        weights.append((current * previous, 2.0 * current / half_width))
        previous = current
    return 1.0 / center, weights


def global_columns(pattern, send_list):
    blocks = pattern.shape[0]
    devices = send_list.shape[0]
    per_device = blocks // devices
    ghost_cap = send_list.shape[2]
    owner_dev = jnp.arange(blocks, dtype=jnp.int32) // per_device
    is_local = pattern < per_device
    ghost_slot = jnp.maximum(pattern - per_device, 0)
    group_num = ghost_slot // ghost_cap
    within = ghost_slot % ghost_cap
    step_table = jnp.array(GHOST_STEPS, dtype=jnp.int32)
    source = owner_dev[:, None] - step_table[group_num]
    valid = (source >= 0) & (source < devices)
    safe_source = jnp.clip(source, 0, devices - 1)
    sent_block = send_list[safe_source, group_num, within]
    ghost_global = safe_source * per_device + sent_block
    local_global = owner_dev[:, None] * per_device + pattern
    chosen = jnp.where(is_local, local_global, jnp.where(valid, ghost_global, blocks))
    return chosen.astype(jnp.int32)


def apply_operator(pair_unit_vector, diagonal, active_f, conductance, columns):
    blocks = columns.shape[0]
    masked = (pair_unit_vector * active_f[:, None]).astype(jnp.bfloat16)
    padded = jnp.concatenate([masked.reshape(blocks, NODES_PER_COLUMN, PROCESS_CASES), jnp.zeros((1, NODES_PER_COLUMN, PROCESS_CASES), jnp.bfloat16)], 0)
    total = jnp.zeros((blocks, NODES_PER_COLUMN, PROCESS_CASES), jnp.float32)
    for tile_k in range(TILES):
        chosen = padded[columns[:, tile_k]].astype(jnp.float32)
        total = total + jnp.einsum("bij,bjr->bir", conductance[:, tile_k].astype(jnp.float32), chosen)
    return diagonal[:, None] * pair_unit_vector + active_f[:, None] * total.reshape(-1, PROCESS_CASES)


def neighbour(field, axis_num, sign):
    size = field.shape[axis_num]
    widths = [(0, 0)] * field.ndim
    widths[axis_num] = (1, 1)
    padded = jnp.pad(field, widths)
    return lax.slice_in_dim(padded, 1 + sign, 1 + sign + size, axis=axis_num)


def mechanics(displacement, lattice_nodes, bond_live):
    moving = displacement.astype(jnp.float32)
    heat = lattice_nodes.astype(jnp.float32)
    live = bond_live.astype(jnp.float32)
    directions = [(0, 1), (1, 1), (2, 1), (0, -1), (1, -1), (2, -1)]

    def stretch_of(axis_num, sign):
        return neighbour(moving, axis_num, sign) - moving - ALPHA_T * 0.5 * (heat + neighbour(heat, axis_num, sign))

    volume_dilatation = jnp.zeros_like(moving)
    for bond_count, (axis_num, sign) in enumerate(directions):
        volume_dilatation = volume_dilatation + live[bond_count][..., None] * stretch_of(axis_num, sign)
    volume_dilatation = volume_dilatation / 6.0
    force = jnp.zeros_like(moving)
    for bond_count, (axis_num, sign) in enumerate(directions):
        series_term = BOND_STIFFNESS * stretch_of(axis_num, sign) + STATE_STIFFNESS * (neighbour(volume_dilatation, axis_num, sign) - volume_dilatation)
        force = force + live[bond_count][..., None] * series_term
    return (moving + STEP_SIZE * force).astype(jnp.bfloat16)


def reference(heat_source, diagonal, active, conductance, pattern, send_list, owner_map, displacement, bond_live):
    columns = global_columns(pattern, send_list)
    active_f = active.astype(jnp.float32)
    first_scale, weights = chebyshev_weights(ITERS)
    residual = heat_source.astype(jnp.float32)
    pair_unit_vector = residual * first_scale
    computed_heat_map = jnp.zeros_like(residual)
    for old_weight, res_weight in weights:
        image = apply_operator(pair_unit_vector, diagonal, active_f, conductance, columns)
        computed_heat_map = computed_heat_map + pair_unit_vector
        residual = residual - image
        pair_unit_vector = old_weight * pair_unit_vector + res_weight * residual
    thermal_profile = (computed_heat_map + pair_unit_vector).astype(jnp.bfloat16)
    desired_quantity = (owner_map[0] * BLK_DEV + owner_map[1]).astype(jnp.int32)
    lattice_nodes = jnp.zeros((PATH_SEGMENTS, NODES_PER_COLUMN, PROCESS_CASES), jnp.bfloat16).at[desired_quantity].set(thermal_profile.reshape(PATH_SEGMENTS, NODES_PER_COLUMN, PROCESS_CASES))
    lattice_nodes = lattice_nodes.reshape(N_ROW, N_COL, BX, BY, NODES_PER_COLUMN, PROCESS_CASES).transpose(0, 2, 1, 3, 4, 5).reshape(X, Y, NODES_PER_COLUMN, PROCESS_CASES)
    moved = mechanics(displacement, lattice_nodes, bond_live)
    return lattice_nodes, moved
```

```python
import functools

import jax
import jax.numpy as jnp
from jax import lax
from jax.experimental import pallas as pl
from jax.experimental.pallas import tpu as pltpu
from jax.sharding import PartitionSpec as P

ITERS = 3
LOWER = 1.0
UPPER = 10.0
ALPHA_T = 0.5
BOND_STIFFNESS = 1.0
STATE_STIFFNESS = 2.0
STEP_SIZE = 0.1
GHOST_STEPS = (1, -1, 2, -2)
SEND_ORDER = (2, 3, 0, 1)
MESH = pl.DeviceIdType.MESH
MIB = 1024 * 1024


def chebyshev_weights(count):
    center = (UPPER + LOWER) / 2.0
    half_width = (UPPER - LOWER) / 2.0
    ratio_value = center / half_width
    previous = 1.0 / ratio_value
    weights = []
    for step_number in range(count):
        current = 1.0 / (2.0 * ratio_value - previous)
        weights.append((current * previous, 2.0 * current / half_width))
        previous = current
    return (1.0 / center, weights)


def chebyshev_kernel(
    pattern,
    send_list,
    route,
    heat,
    active,
    diagonal,
    conductance,
    out,
    tiles,
    ext0,
    ext1,
    ext2,
    masked,
    outgoing,
    residual,
    direction,
    total,
    active_wide,
    diagonal_wide,
    tile_sem,
    send_sem,
    recv_sem,
):
    rows, cols = lax.axis_size("row"), lax.axis_size("col")
    devices = rows * cols
    me = lax.axis_index("row") * cols + lax.axis_index("col")
    blocks, length, cases = heat.shape
    tile_count = tiles.shape[1]
    cap = outgoing.shape[0] // len(GHOST_STEPS)
    exts = (ext0, ext1, ext2)
    first_scale, weights = chebyshev_weights(ITERS)

    tile_copy = pltpu.make_async_copy(conductance, tiles, tile_sem)
    tile_copy.start()

    def inside(index):
        return jnp.logical_and(index >= 0, index < devices)

    def place(index):
        return (lax.div(index, cols), lax.rem(index, cols))

    barrier = pltpu.get_barrier_semaphore()
    for step in GHOST_STEPS:

        @pl.when(inside(me + step))
        def _():
            pl.semaphore_signal(barrier, inc=1, device_id=place(me + step), device_id_type=MESH)

    def ghost_copy(it, group):
        return pltpu.make_async_remote_copy(
            src_ref=outgoing.at[pl.ds(group * cap, cap)],
            dst_ref=exts[it].at[pl.ds(blocks + group * cap, cap)],
            send_sem=send_sem.at[it, group],
            recv_sem=recv_sem.at[it, group],
            device_id=place(me + GHOST_STEPS[group]),
            device_id_type=MESH,
        )

    wide = jnp.concatenate([active[...], diagonal[...]], axis=0).T
    for b in range(blocks):
        column = jnp.broadcast_to(wide[:, b : b + 1], (length, cases))
        active_wide[b] = column.astype(jnp.bfloat16)

    @pl.loop(0, blocks)
    def _(b):
        source = heat[b].astype(jnp.float32)
        start = source * first_scale
        residual[b] = source
        direction[b] = start
        value = (start * active_wide[b].astype(jnp.float32)).astype(jnp.bfloat16)
        masked[b] = value
        ext0[b] = value

    peers = sum(jnp.where(inside(me + step), 1, 0) for step in GHOST_STEPS)
    pl.semaphore_wait(barrier, peers)

    for it in range(ITERS):
        ext = exts[it]
        for group in SEND_ORDER:
            step = GHOST_STEPS[group]
            if it > 0:

                @pl.when(inside(me + step))
                def _():
                    ghost_copy(it - 1, group).wait_send()

            @pl.loop(0, cap)
            def _(j):
                outgoing[group * cap + j] = masked[send_list[group * cap + j]]

            @pl.when(inside(me + step))
            def _():
                ghost_copy(it, group).start()

        for group, step in enumerate(GHOST_STEPS):

            @pl.when(jnp.logical_not(inside(me - step)))
            def _():
                ext[pl.ds(blocks + group * cap, cap)] = jnp.zeros(
                    (cap, length, cases), jnp.bfloat16
                )

        if it == 0:
            for b in range(blocks):
                diagonal_wide[b] = jnp.broadcast_to(
                    wide[:, blocks + b : blocks + b + 1], (length, cases)
                )
            tile_copy.wait()

        @pl.loop(0, blocks)
        def _(b):
            own = jnp.dot(tiles[b, 0], masked[b], preferred_element_type=jnp.float32)
            held = direction[b]
            residual[b] = (
                residual[b] - diagonal_wide[b] * held - active_wide[b].astype(jnp.float32) * own
            )
            if it == 0:
                total[b] = held
            else:
                total[b] = total[b] + held

        for group, step in enumerate(GHOST_STEPS):

            @pl.when(inside(me - step))
            def _():
                ghost_copy(it, group).wait_recv()

        old_weight, res_weight = weights[it]
        unroll = 2

        @pl.loop(0, blocks // unroll)
        def _(pair):
            for part in range(unroll):
                b = pair * unroll + part
                chosen = [ext[blocks + b]]
                for k in range(2, tile_count):
                    chosen.append(ext[pattern[b * tile_count + k]])
                row = jnp.concatenate([tiles[b, k] for k in range(1, tile_count)], axis=1)
                far = jnp.dot(
                    row, jnp.concatenate(chosen, axis=0), preferred_element_type=jnp.float32
                )
                mask = active_wide[b].astype(jnp.float32)
                left = residual[b] - mask * far
                held = old_weight * direction[b] + res_weight * left
                if it < ITERS - 1:
                    residual[b] = left
                    direction[b] = held
                    value = (held * mask).astype(jnp.bfloat16)
                    masked[b] = value
                    exts[it + 1][b] = value
                else:
                    masked[b] = (total[b] + held).astype(jnp.bfloat16)

    @pl.loop(0, out.shape[0])
    def _(j):
        out[j] = masked[route[j]]

    for group, step in enumerate(GHOST_STEPS):

        @pl.when(inside(me + step))
        def _():
            ghost_copy(ITERS - 1, group).wait_send()


def chebyshev(pattern, send_list, route, heat, active, diagonal, conductance):
    blocks, length, cases = heat.shape
    tile_count = conductance.shape[1]
    ghosts = send_list.shape[0]
    smem = pl.BlockSpec(memory_space=pltpu.SMEM)
    vmem = pl.BlockSpec(memory_space=pltpu.VMEM)
    hbm = pl.BlockSpec(memory_space=pl.ANY)
    state = pltpu.VMEM((blocks, length, cases), jnp.float32)
    ext = pltpu.VMEM((blocks + ghosts, length, cases), jnp.bfloat16)
    half = pltpu.VMEM((blocks, length, cases), jnp.bfloat16)
    return pl.pallas_call(
        chebyshev_kernel,
        out_shape=jax.ShapeDtypeStruct((route.shape[0], length, cases), jnp.bfloat16),
        in_specs=[smem, smem, smem, vmem, vmem, vmem, hbm],
        out_specs=vmem,
        scratch_shapes=[
            pltpu.VMEM(conductance.shape, jnp.bfloat16),
            ext,
            ext,
            ext,
            half,
            pltpu.VMEM((ghosts, length, cases), jnp.bfloat16),
            state,
            state,
            state,
            half,
            state,
            pltpu.SemaphoreType.DMA,
            pltpu.SemaphoreType.DMA((ITERS, len(GHOST_STEPS))),
            pltpu.SemaphoreType.DMA((ITERS, len(GHOST_STEPS))),
        ],
        compiler_params=pltpu.CompilerParams(
            collective_id=0, has_side_effects=True, vmem_limit_bytes=58 * MIB
        ),
        name="chebyshev",
    )(pattern, send_list, route, heat, active, diagonal, conductance)


def edges(field, axis, dim):
    size, length = lax.axis_size(axis), field.shape[dim]
    up = [(i, i + 1) for i in range(size - 1)]
    down = [(j, i) for i, j in up]
    last = lax.slice_in_dim(field, length - 1, length, axis=dim)
    leading = lax.slice_in_dim(field, 0, 1, axis=dim)
    return lax.ppermute(last, axis, up), lax.ppermute(leading, axis, down)


def bond_sum(field, live):
    sent = field.astype(jnp.bfloat16)
    low_x, high_x = edges(sent, "row", 0)
    low_y, high_y = edges(sent, "col", 1)
    wide_x = jnp.concatenate([low_x.astype(jnp.float32), field, high_x.astype(jnp.float32)], 0)
    wide_y = jnp.concatenate([low_y.astype(jnp.float32), field, high_y.astype(jnp.float32)], 1)
    wide_z = jnp.pad(field, ((0, 0), (0, 0), (1, 1), (0, 0)))
    return (
        live[0] * wide_x[2:]
        + live[1] * wide_y[:, 2:]
        + live[2] * wide_z[:, :, 2:]
        + live[3] * wide_x[:-2]
        + live[4] * wide_y[:, :-2]
        + live[5] * wide_z[:, :, :-2]
    )


def local(
    heat_source,
    diagonal,
    active,
    conductance,
    pattern,
    send_list,
    owner_map,
    displacement,
    bond_live,
):
    blocks, tile_count, length = conductance.shape[:3]
    cases = heat_source.shape[1]
    devices = lax.axis_size(("row", "col"))
    me = lax.axis_index(("row", "col"))
    cap = max(1, blocks // devices)

    slots = jnp.arange(blocks, dtype=jnp.int32)
    mine = lax.dynamic_slice_in_dim(owner_map, me * blocks, blocks, axis=1)
    my_distance = (mine[0] - me + devices) % devices
    of_slot = mine[1][None, :] == slots[:, None]
    block_of = jnp.sum(jnp.where(of_slot, slots[None, :], 0), axis=1)
    distance = jnp.sum(jnp.where(of_slot, my_distance[None, :], 0), axis=1)
    rank = jnp.sum(
        ((distance[:, None] == distance[None, :]) & (slots[None, :] < slots[:, None])).astype(
            jnp.int32
        ),
        axis=1,
    )
    target = ((me + distance) % devices) * cap + rank
    places = jnp.arange(devices * cap, dtype=jnp.int32)
    route = jnp.sum(jnp.where(target[None, :] == places[:, None], block_of[None, :], 0), axis=1)
    source_row = ((me - distance + devices) % devices) * cap + rank

    outgoing = chebyshev(
        pattern.reshape(-1),
        send_list.reshape(-1),
        route,
        heat_source.reshape(blocks, length, cases),
        active.astype(jnp.float32).reshape(blocks, length),
        diagonal.reshape(blocks, length),
        conductance,
    )
    arrived = lax.all_to_all(outgoing, ("row", "col"), split_axis=0, concat_axis=0, tiled=True)
    bricks = arrived[source_row].reshape(displacement.shape)

    live = bond_live.astype(jnp.float32)[..., None]
    count = jnp.sum(live, axis=0)
    moving = displacement.astype(jnp.float32)
    heat = (ALPHA_T * 0.5) * bricks.astype(jnp.float32)
    dilatation = (bond_sum(moving - heat, live) - count * (moving + heat)) / 6.0
    force = BOND_STIFFNESS * 6.0 * dilatation + STATE_STIFFNESS * (
        bond_sum(dilatation, live) - count * dilatation
    )
    moved = (moving + STEP_SIZE * force).astype(jnp.bfloat16)
    return (bricks, moved)


def solution(mesh):
    return jax.shard_map(
        local,
        mesh=mesh,
        in_specs=(
            P(("row", "col"), None),
            P(("row", "col")),
            P(("row", "col")),
            P(("row", "col"), None, None, None),
            P(("row", "col"), None),
            P(("row", "col"), None, None),
            P(),
            P("row", "col", None, None),
            P(None, "row", "col", None),
        ),
        out_specs=(P("row", "col", None, None), P("row", "col", None, None)),
        check_vma=False,
    )
```

```python
import jax
import jax.numpy as jnp
from jax import lax
from jax.experimental import pallas as pl
from jax.experimental.pallas import tpu as pltpu
from jax.sharding import PartitionSpec as P

ITERS = 3
LOWER = 1.0
UPPER = 10.0
ALPHA_T = 0.5
BOND_STIFFNESS = 1.0
STATE_STIFFNESS = 2.0
STEP_SIZE = 0.1
GHOST_STEPS = (1, -1, 2, -2)
SEND_ORDER = (2, 3, 0, 1)
MESH = pl.DeviceIdType.MESH
MIB = 1024 * 1024


def chebyshev_weights(count):
    center = (UPPER + LOWER) / 2.0
    half_width = (UPPER - LOWER) / 2.0
    ratio_value = center / half_width
    previous = 1.0 / ratio_value
    weights = []
    for step_number in range(count):
        current = 1.0 / (2.0 * ratio_value - previous)
        weights.append((current * previous, 2.0 * current / half_width))
        previous = current
    return (1.0 / center, weights)


def chebyshev_kernel(
    pattern,
    send_list,
    route,
    heat,
    active,
    diagonal,
    conductance,
    out,
    tiles,
    ext0,
    ext1,
    ext2,
    masked,
    outgoing,
    residual,
    direction,
    total,
    active_wide,
    diagonal_wide,
    tile_sem,
    send_sem,
    recv_sem,
):
    rows, cols = lax.axis_size("row"), lax.axis_size("col")
    devices = rows * cols
    me = lax.axis_index("row") * cols + lax.axis_index("col")
    blocks, length, cases = heat.shape
    tile_count = tiles.shape[1]
    cap = outgoing.shape[0] // len(GHOST_STEPS)
    exts = (ext0, ext1, ext2)
    first_scale, weights = chebyshev_weights(ITERS)

    tile_copy = pltpu.make_async_copy(conductance, tiles, tile_sem)
    tile_copy.start()

    def inside(index):
        return jnp.logical_and(index >= 0, index < devices)

    def place(index):
        return (lax.div(index, cols), lax.rem(index, cols))

    barrier = pltpu.get_barrier_semaphore()
    for step in GHOST_STEPS:

        @pl.when(inside(me + step))
        def _():
            pl.semaphore_signal(barrier, inc=1, device_id=place(me + step), device_id_type=MESH)

    def ghost_copy(it, group):
        return pltpu.make_async_remote_copy(
            src_ref=outgoing.at[pl.ds(group * cap, cap)],
            dst_ref=exts[it].at[pl.ds(blocks + group * cap, cap)],
            send_sem=send_sem.at[it, group],
            recv_sem=recv_sem.at[it, group],
            device_id=place(me + GHOST_STEPS[group]),
            device_id_type=MESH,
        )

    wide = jnp.concatenate([active[...], diagonal[...]], axis=0).T
    for b in range(blocks):
        column = jnp.broadcast_to(wide[:, b : b + 1], (length, cases))
        active_wide[b] = column.astype(jnp.bfloat16)

    @pl.loop(0, blocks)
    def _(b):
        source = heat[b].astype(jnp.float32)
        start = source * first_scale
        residual[b] = source
        direction[b] = start
        value = (start * active_wide[b].astype(jnp.float32)).astype(jnp.bfloat16)
        masked[b] = value
        ext0[b] = value

    peers = sum(jnp.where(inside(me + step), 1, 0) for step in GHOST_STEPS)
    pl.semaphore_wait(barrier, peers)

    for it in range(ITERS):
        ext = exts[it]
        for group in SEND_ORDER:
            step = GHOST_STEPS[group]
            if it > 0:

                @pl.when(inside(me + step))
                def _():
                    ghost_copy(it - 1, group).wait_send()

            @pl.loop(0, cap)
            def _(j):
                outgoing[group * cap + j] = masked[send_list[group * cap + j]]

            @pl.when(inside(me + step))
            def _():
                ghost_copy(it, group).start()

        for group, step in enumerate(GHOST_STEPS):

            @pl.when(jnp.logical_not(inside(me - step)))
            def _():
                ext[pl.ds(blocks + group * cap, cap)] = jnp.zeros(
                    (cap, length, cases), jnp.bfloat16
                )

        if it == 0:
            for b in range(blocks):
                diagonal_wide[b] = jnp.broadcast_to(
                    wide[:, blocks + b : blocks + b + 1], (length, cases)
                )
            tile_copy.wait()

        @pl.loop(0, blocks)
        def _(b):
            own = jnp.dot(tiles[b, 0], masked[b], preferred_element_type=jnp.float32)
            held = direction[b]
            residual[b] = (
                residual[b] - diagonal_wide[b] * held - active_wide[b].astype(jnp.float32) * own
            )
            if it == 0:
                total[b] = held
            else:
                total[b] = total[b] + held

        for group, step in enumerate(GHOST_STEPS):

            @pl.when(inside(me - step))
            def _():
                ghost_copy(it, group).wait_recv()

        old_weight, res_weight = weights[it]
        unroll = 2

        @pl.loop(0, blocks // unroll)
        def _(pair):
            for part in range(unroll):
                b = pair * unroll + part
                chosen = [ext[blocks + b]]
                for k in range(2, tile_count):
                    chosen.append(ext[pattern[b * tile_count + k]])
                row = jnp.concatenate([tiles[b, k] for k in range(1, tile_count)], axis=1)
                far = jnp.dot(
                    row, jnp.concatenate(chosen, axis=0), preferred_element_type=jnp.float32
                )
                mask = active_wide[b].astype(jnp.float32)
                left = residual[b] - mask * far
                held = old_weight * direction[b] + res_weight * left
                if it < ITERS - 1:
                    residual[b] = left
                    direction[b] = held
                    value = (held * mask).astype(jnp.bfloat16)
                    masked[b] = value
                    exts[it + 1][b] = value
                else:
                    masked[b] = (total[b] + held).astype(jnp.bfloat16)

    @pl.loop(0, out.shape[0])
    def _(j):
        out[j] = masked[route[j]]

    for group, step in enumerate(GHOST_STEPS):

        @pl.when(inside(me + step))
        def _():
            ghost_copy(ITERS - 1, group).wait_send()


def chebyshev(pattern, send_list, route, heat, active, diagonal, conductance):
    blocks, length, cases = heat.shape
    tile_count = conductance.shape[1]
    ghosts = send_list.shape[0]
    smem = pl.BlockSpec(memory_space=pltpu.SMEM)
    vmem = pl.BlockSpec(memory_space=pltpu.VMEM)
    hbm = pl.BlockSpec(memory_space=pl.ANY)
    state = pltpu.VMEM((blocks, length, cases), jnp.float32)
    ext = pltpu.VMEM((blocks + ghosts, length, cases), jnp.bfloat16)
    half = pltpu.VMEM((blocks, length, cases), jnp.bfloat16)
    return pl.pallas_call(
        chebyshev_kernel,
        out_shape=jax.ShapeDtypeStruct((route.shape[0], length, cases), jnp.bfloat16),
        in_specs=[smem, smem, smem, vmem, vmem, vmem, hbm],
        out_specs=vmem,
        scratch_shapes=[
            pltpu.VMEM(conductance.shape, jnp.bfloat16),
            ext,
            ext,
            ext,
            half,
            pltpu.VMEM((ghosts, length, cases), jnp.bfloat16),
            state,
            state,
            state,
            half,
            state,
            pltpu.SemaphoreType.DMA,
            pltpu.SemaphoreType.DMA((ITERS, len(GHOST_STEPS))),
            pltpu.SemaphoreType.DMA((ITERS, len(GHOST_STEPS))),
        ],
        compiler_params=pltpu.CompilerParams(
            collective_id=0, has_side_effects=True, vmem_limit_bytes=58 * MIB
        ),
        name="chebyshev",
    )(pattern, send_list, route, heat, active, diagonal, conductance)


def mechanics_kernel(
    source_row,
    arrived,
    displacement,
    bond_live,
    bricks,
    moved,
    stretch,
    dilation,
    live,
    send_x,
    send_y,
    recv_x,
    recv_y,
    send_sem,
    recv_sem,
):
    sizes = (lax.axis_size("row"), lax.axis_size("col"))
    here = (lax.axis_index("row"), lax.axis_index("col"))
    columns_x, columns_y, length, cases = displacement.shape
    sends, recvs = ((send_x, send_y), (recv_x, recv_y))
    bonds = ((0, 3), (1, 4))
    quarter = ALPHA_T * 0.5

    def beside(axis, side):
        return here[axis] + (1 if side == 0 else -1)

    def present(axis, side):
        index = beside(axis, side)
        return jnp.logical_and(index >= 0, index < sizes[axis])

    def place(axis, side):
        index = beside(axis, side)
        return (index, here[1]) if axis == 0 else (here[0], index)

    def edge_copy(turn, axis, side):
        return pltpu.make_async_remote_copy(
            src_ref=sends[axis].at[turn, side],
            dst_ref=recvs[axis].at[turn, 1 - side],
            send_sem=send_sem.at[turn, axis, side],
            recv_sem=recv_sem.at[turn, axis, 1 - side],
            device_id=place(axis, side),
            device_id_type=MESH,
        )

    pairs = [(axis, side) for axis in (1, 0) for side in (0, 1)]
    barrier = pltpu.get_barrier_semaphore()
    for axis, side in pairs:

        @pl.when(present(axis, side))
        def _():
            pl.semaphore_signal(barrier, inc=1, device_id=place(axis, side), device_id_type=MESH)

    def fetch(x, y):
        temperature = arrived[source_row[x * columns_y + y]]
        bricks[x, y] = temperature
        value = displacement[x, y].astype(jnp.float32) - quarter * temperature.astype(jnp.float32)
        stretch[x + 1, y] = value
        return value.astype(jnp.bfloat16)

    def launch(turn, axis):
        for side in (0, 1):

            @pl.when(present(axis, side))
            def _():
                edge_copy(turn, axis, side).start()

    def arrive(turn, axis, side, add):
        @pl.when(present(axis, side))
        def _():
            edge_copy(turn, axis, 1 - side).wait_recv()
            if axis == 0:
                for y in range(columns_y):
                    add(columns_x - 1 if side == 0 else 0, y, y)
            else:

                @pl.loop(0, columns_x)
                def _(x):
                    add(x, columns_y - 1 if side == 0 else 0, x)

    def bond_sum(field, x, y):
        middle = field[x + 1, y]
        bond = [live[d, x * columns_y + y].astype(jnp.float32) for d in range(6)]
        result = bond[0] * field[x + 2, y] + bond[3] * field[x, y]
        result = result + bond[2] * pltpu.roll(middle, length - 1, 0)
        result = result + bond[5] * pltpu.roll(middle, 1, 0)
        if y + 1 < columns_y:
            result = result + bond[1] * field[x + 1, y + 1]
        if y > 0:
            result = result + bond[4] * field[x + 1, y - 1]
        count = bond[0] + bond[1] + bond[2] + bond[3] + bond[4] + bond[5]
        return middle, result, count

    @pl.loop(0, columns_x)
    def _(x):
        send_y[0, 0, x] = fetch(x, columns_y - 1)
        send_y[0, 1, x] = fetch(x, 0)

    peers = sum(jnp.where(present(axis, side), 1, 0) for axis, side in pairs)
    pl.semaphore_wait(barrier, peers)
    launch(0, 1)

    @pl.loop(0, columns_x)
    def _(x):
        for y in range(1, columns_y - 1):
            fetch(x, y)

    for y in range(columns_y):
        send_x[0, 0, y] = stretch[columns_x, y].astype(jnp.bfloat16)
        send_x[0, 1, y] = stretch[1, y].astype(jnp.bfloat16)
    launch(0, 0)

    nothing = jnp.zeros((length, cases), jnp.float32)
    for field in (stretch, dilation):
        for y in range(columns_y):
            field[0, y] = nothing
            field[columns_x + 1, y] = nothing

    columns = columns_x * columns_y
    for first in range(0, 6 * columns, length):
        turned = bond_live[first : first + length].astype(jnp.float32).T
        for j in range(turned.shape[1]):
            live[(first + j) // columns, (first + j) % columns] = jnp.broadcast_to(
                turned[:, j : j + 1], (length, cases)
            ).astype(jnp.bfloat16)

    @pl.loop(0, columns_x)
    def _(x):
        for y in range(columns_y):
            _, result, count = bond_sum(stretch, x, y)
            other = displacement[x, y].astype(jnp.float32) + quarter * bricks[x, y].astype(
                jnp.float32
            )
            dilation[x + 1, y] = (result - count * other) * (1.0 / 6.0)

    def complete(axis, side):
        def add(x, y, at):
            bond = live[bonds[axis][side], x * columns_y + y].astype(jnp.float32)
            value = recvs[axis][0, side, at].astype(jnp.float32)
            dilation[x + 1, y] = dilation[x + 1, y] + bond * value * (1.0 / 6.0)

        arrive(0, axis, side, add)

    for axis, side in reversed(pairs):
        complete(axis, side)

    @pl.loop(0, columns_x)
    def _(x):
        send_y[1, 0, x] = dilation[x + 1, columns_y - 1].astype(jnp.bfloat16)
        send_y[1, 1, x] = dilation[x + 1, 0].astype(jnp.bfloat16)

    launch(1, 1)
    for y in range(columns_y):
        send_x[1, 0, y] = dilation[columns_x, y].astype(jnp.bfloat16)
        send_x[1, 1, y] = dilation[1, y].astype(jnp.bfloat16)
    launch(1, 0)

    @pl.loop(0, columns_x)
    def _(x):
        for y in range(columns_y):
            middle, result, count = bond_sum(dilation, x, y)
            force = (6.0 * BOND_STIFFNESS) * middle + STATE_STIFFNESS * (result - count * middle)
            value = displacement[x, y].astype(jnp.float32) + STEP_SIZE * force
            stretch[x + 1, y] = value
            if 0 < y < columns_y - 1:
                moved[x, y] = value.astype(jnp.bfloat16)

    def finish(axis, side):
        def add(x, y, at):
            bond = live[bonds[axis][side], x * columns_y + y].astype(jnp.float32)
            value = recvs[axis][1, side, at].astype(jnp.float32)
            value = stretch[x + 1, y] + (STEP_SIZE * STATE_STIFFNESS) * (bond * value)
            stretch[x + 1, y] = value
            if axis == 0 and 0 < y < columns_y - 1:
                moved[x, y] = value.astype(jnp.bfloat16)

        arrive(1, axis, side, add)

    for axis, side in reversed(pairs):
        finish(axis, side)

    @pl.loop(0, columns_x)
    def _(x):
        for y in (0, columns_y - 1):
            moved[x, y] = stretch[x + 1, y].astype(jnp.bfloat16)

    for turn in (0, 1):
        for axis, side in pairs:

            @pl.when(present(axis, side))
            def _():
                edge_copy(turn, axis, side).wait_send()


def mechanics(source_row, arrived, displacement, bond_live):
    columns_x, columns_y, length, cases = displacement.shape
    columns = columns_x * columns_y
    vmem = pl.BlockSpec(memory_space=pltpu.VMEM)
    field = pltpu.VMEM((columns_x + 2, columns_y, length, cases), jnp.float32)
    edge_x = pltpu.VMEM((2, 2, columns_y, length, cases), jnp.bfloat16)
    edge_y = pltpu.VMEM((2, 2, columns_x, length, cases), jnp.bfloat16)
    out = jax.ShapeDtypeStruct(displacement.shape, jnp.bfloat16)
    return pl.pallas_call(
        mechanics_kernel,
        out_shape=(out, out),
        in_specs=[pl.BlockSpec(memory_space=pltpu.SMEM), vmem, vmem, vmem],
        out_specs=(vmem, vmem),
        scratch_shapes=[
            field,
            field,
            pltpu.VMEM((6, columns, length, cases), jnp.bfloat16),
            edge_x,
            edge_y,
            edge_x,
            edge_y,
            pltpu.SemaphoreType.DMA((2, 2, 2)),
            pltpu.SemaphoreType.DMA((2, 2, 2)),
        ],
        compiler_params=pltpu.CompilerParams(
            collective_id=1, has_side_effects=True, vmem_limit_bytes=50 * MIB
        ),
        name="mechanics",
    )(source_row, arrived, displacement, bond_live.reshape(6 * columns, length))


def local(
    heat_source,
    diagonal,
    active,
    conductance,
    pattern,
    send_list,
    owner_map,
    displacement,
    bond_live,
):
    blocks, tile_count, length = conductance.shape[:3]
    cases = heat_source.shape[1]
    devices = lax.axis_size(("row", "col"))
    me = lax.axis_index(("row", "col"))
    cap = max(1, blocks // devices)

    slots = jnp.arange(blocks, dtype=jnp.int32)
    mine = lax.dynamic_slice_in_dim(owner_map, me * blocks, blocks, axis=1)
    my_distance = (mine[0] - me + devices) % devices
    of_slot = mine[1][None, :] == slots[:, None]
    block_of = jnp.sum(jnp.where(of_slot, slots[None, :], 0), axis=1)
    distance = jnp.sum(jnp.where(of_slot, my_distance[None, :], 0), axis=1)
    rank = jnp.sum(
        ((distance[:, None] == distance[None, :]) & (slots[None, :] < slots[:, None])).astype(
            jnp.int32
        ),
        axis=1,
    )
    target = ((me + distance) % devices) * cap + rank
    places = jnp.arange(devices * cap, dtype=jnp.int32)
    route = jnp.sum(jnp.where(target[None, :] == places[:, None], block_of[None, :], 0), axis=1)
    source_row = ((me - distance + devices) % devices) * cap + rank

    outgoing = chebyshev(
        pattern.reshape(-1),
        send_list.reshape(-1),
        route,
        heat_source.reshape(blocks, length, cases),
        active.astype(jnp.float32).reshape(blocks, length),
        diagonal.reshape(blocks, length),
        conductance,
    )
    arrived = lax.all_to_all(outgoing, ("row", "col"), split_axis=0, concat_axis=0, tiled=True)
    return mechanics(source_row, arrived, displacement, bond_live)


def solution(mesh):
    return jax.shard_map(
        local,
        mesh=mesh,
        in_specs=(
            P(("row", "col"), None),
            P(("row", "col")),
            P(("row", "col")),
            P(("row", "col"), None, None, None),
            P(("row", "col"), None),
            P(("row", "col"), None, None),
            P(),
            P("row", "col", None, None),
            P(None, "row", "col", None),
        ),
        out_specs=(P("row", "col", None, None), P("row", "col", None, None)),
        check_vma=False,
    )
```

```python
import jax
import jax.numpy as jnp
from jax import lax
from jax.experimental import pallas as pl
from jax.experimental.pallas import tpu as pltpu
from jax.sharding import PartitionSpec as P

ITERS = 3
LOWER = 1.0
UPPER = 10.0
ALPHA_T = 0.5
BOND_STIFFNESS = 1.0
STATE_STIFFNESS = 2.0
STEP_SIZE = 0.1
GHOST_STEPS = (1, -1, 2, -2)
SEND_ORDER = (2, 3, 0, 1)
MESH = pl.DeviceIdType.MESH
MIB = 1024 * 1024


def chebyshev_weights(count):
    center = (UPPER + LOWER) / 2.0
    half_width = (UPPER - LOWER) / 2.0
    ratio_value = center / half_width
    previous = 1.0 / ratio_value
    weights = []
    for step_number in range(count):
        current = 1.0 / (2.0 * ratio_value - previous)
        weights.append((current * previous, 2.0 * current / half_width))
        previous = current
    return (1.0 / center, weights)


def chebyshev_kernel(
    pattern,
    send_list,
    route,
    heat,
    active,
    diagonal,
    conductance,
    out,
    tiles,
    ext0,
    ext1,
    ext2,
    masked,
    outgoing,
    residual,
    direction,
    total,
    active_wide,
    diagonal_wide,
    tile_sem,
    send_sem,
    recv_sem,
    brick_send_sem,
    brick_recv_sem,
    kept_sem,
    stage,
):
    rows, cols = lax.axis_size("row"), lax.axis_size("col")
    devices = rows * cols
    me = lax.axis_index("row") * cols + lax.axis_index("col")
    blocks, length, cases = heat.shape
    tile_count = tiles.shape[1]
    cap = outgoing.shape[0] // len(GHOST_STEPS)
    exts = (ext0, ext1, ext2)
    first_scale, weights = chebyshev_weights(ITERS)

    tile_copy = pltpu.make_async_copy(conductance, tiles, tile_sem)
    tile_copy.start()

    def inside(index):
        return jnp.logical_and(index >= 0, index < devices)

    def place(index):
        return (lax.div(index, cols), lax.rem(index, cols))

    barrier = pltpu.get_barrier_semaphore()

    @pl.loop(1, devices)
    def _(k):
        pl.semaphore_signal(
            barrier, inc=1, device_id=place(lax.rem(me + k, devices)), device_id_type=MESH
        )

    def ghost_copy(it, group):
        return pltpu.make_async_remote_copy(
            src_ref=outgoing.at[pl.ds(group * cap, cap)],
            dst_ref=exts[it].at[pl.ds(blocks + group * cap, cap)],
            send_sem=send_sem.at[it, group],
            recv_sem=recv_sem.at[it, group],
            device_id=place(me + GHOST_STEPS[group]),
            device_id_type=MESH,
        )

    wide = jnp.concatenate([active[...].astype(jnp.float32), diagonal[...]], axis=0).T
    for b in range(blocks):
        column = jnp.broadcast_to(wide[:, b : b + 1], (length, cases))
        active_wide[b] = column.astype(jnp.bfloat16)

    @pl.loop(0, blocks)
    def _(b):
        source = heat[b].astype(jnp.float32)
        start = source * first_scale
        residual[b] = source
        direction[b] = start
        value = (start * active_wide[b].astype(jnp.float32)).astype(jnp.bfloat16)
        masked[b] = value
        ext0[b] = value

    pl.semaphore_wait(barrier, devices - 1)

    for it in range(ITERS):
        ext = exts[it]
        for group in SEND_ORDER:
            step = GHOST_STEPS[group]
            if it > 0:

                @pl.when(inside(me + step))
                def _():
                    ghost_copy(it - 1, group).wait_send()

            @pl.loop(0, cap)
            def _(j):
                outgoing[group * cap + j] = masked[send_list[0, group, j]]

            @pl.when(inside(me + step))
            def _():
                ghost_copy(it, group).start()

        for group, step in enumerate(GHOST_STEPS):

            @pl.when(jnp.logical_not(inside(me - step)))
            def _():
                ext[pl.ds(blocks + group * cap, cap)] = jnp.zeros(
                    (cap, length, cases), jnp.bfloat16
                )

        if it == 0:
            for b in range(blocks):
                diagonal_wide[b] = jnp.broadcast_to(
                    wide[:, blocks + b : blocks + b + 1], (length, cases)
                )
            tile_copy.wait()

        @pl.loop(0, blocks)
        def _(b):
            own = jnp.dot(tiles[b, 0], masked[b], preferred_element_type=jnp.float32)
            held = direction[b]
            residual[b] = (
                residual[b] - diagonal_wide[b] * held - active_wide[b].astype(jnp.float32) * own
            )
            if it == 0:
                total[b] = held
            else:
                total[b] = total[b] + held

        for group, step in enumerate(GHOST_STEPS):

            @pl.when(inside(me - step))
            def _():
                ghost_copy(it, group).wait_recv()

        old_weight, res_weight = weights[it]
        unroll = 4

        @pl.loop(0, blocks // unroll)
        def _(pair):
            for part in range(unroll):
                b = pair * unroll + part
                chosen = [ext[blocks + b]]
                for k in range(2, tile_count):
                    chosen.append(ext[pattern[b, k]])
                row = jnp.concatenate([tiles[b, k] for k in range(1, tile_count)], axis=1)
                far = jnp.dot(
                    row, jnp.concatenate(chosen, axis=0), preferred_element_type=jnp.float32
                )
                mask = active_wide[b].astype(jnp.float32)
                left = residual[b] - mask * far
                held = old_weight * direction[b] + res_weight * left
                if it < ITERS - 1:
                    residual[b] = left
                    direction[b] = held
                    value = (held * mask).astype(jnp.bfloat16)
                    masked[b] = value
                    exts[it + 1][b] = value
                else:
                    masked[b] = (total[b] + held).astype(jnp.bfloat16)

    each = stage.shape[0] // devices

    def pick(index):
        for j in range(each):
            stage[index * each + j] = masked[route[index * each + j]]

    def brick_copy(source, owner, index):
        return pltpu.make_async_remote_copy(
            src_ref=stage.at[pl.ds(source * each, each)],
            dst_ref=out.at[pl.ds(owner * each, each)],
            send_sem=brick_send_sem.at[source],
            recv_sem=brick_recv_sem.at[owner],
            device_id=place(index),
            device_id_type=MESH,
        )

    @pl.loop(1, devices)
    def _(k):
        index = lax.rem(me + k, devices)
        pick(index)
        brick_copy(index, me, index).start()

    pick(me)
    own_rows = pl.ds(me * each, each)
    kept = pltpu.make_async_copy(stage.at[own_rows], out.at[own_rows], kept_sem)
    kept.start()
    kept.wait()

    @pl.loop(1, devices)
    def _(k):
        index = lax.rem(me + k, devices)
        brick_copy(index, me, index).wait_send()

    @pl.loop(1, devices)
    def _(k):
        index = lax.rem(me + devices - k, devices)
        brick_copy(index, index, index).wait_recv()

    for group, step in enumerate(GHOST_STEPS):

        @pl.when(inside(me + step))
        def _():
            ghost_copy(ITERS - 1, group).wait_send()


def chebyshev(pattern, send_list, route, heat, active, diagonal, conductance):
    blocks, length, cases = heat.shape
    tile_count = conductance.shape[1]
    ghosts = send_list.shape[1] * send_list.shape[2]
    devices = lax.axis_size(("row", "col"))
    smem = pl.BlockSpec(memory_space=pltpu.SMEM)
    vmem = pl.BlockSpec(memory_space=pltpu.VMEM)
    hbm = pl.BlockSpec(memory_space=pl.ANY)
    state = pltpu.VMEM((blocks, length, cases), jnp.float32)
    ext = pltpu.VMEM((blocks + ghosts, length, cases), jnp.bfloat16)
    half = pltpu.VMEM((blocks, length, cases), jnp.bfloat16)
    return pl.pallas_call(
        chebyshev_kernel,
        out_shape=jax.ShapeDtypeStruct((route.shape[0], length, cases), jnp.bfloat16),
        in_specs=[smem, smem, smem, vmem, vmem, vmem, hbm],
        out_specs=hbm,
        scratch_shapes=[
            pltpu.VMEM(conductance.shape, jnp.bfloat16),
            ext,
            ext,
            ext,
            half,
            pltpu.VMEM((ghosts, length, cases), jnp.bfloat16),
            state,
            state,
            state,
            half,
            state,
            pltpu.SemaphoreType.DMA,
            pltpu.SemaphoreType.DMA((ITERS, len(GHOST_STEPS))),
            pltpu.SemaphoreType.DMA((ITERS, len(GHOST_STEPS))),
            pltpu.SemaphoreType.DMA((devices,)),
            pltpu.SemaphoreType.DMA((devices,)),
            pltpu.SemaphoreType.DMA,
            pltpu.VMEM((route.shape[0], length, cases), jnp.bfloat16),
        ],
        compiler_params=pltpu.CompilerParams(
            collective_id=0, has_side_effects=True, vmem_limit_bytes=58 * MIB
        ),
        name="chebyshev",
    )(pattern, send_list, route, heat, active, diagonal, conductance)


def mechanics_kernel(
    source_row,
    arrived,
    displacement,
    bond_live,
    bricks,
    moved,
    stretch,
    dilation,
    live,
    send_x,
    send_y,
    recv_x,
    recv_y,
    send_sem,
    recv_sem,
):
    sizes = (lax.axis_size("row"), lax.axis_size("col"))
    here = (lax.axis_index("row"), lax.axis_index("col"))
    columns_x, columns_y, length, cases = displacement.shape
    sends, recvs = ((send_x, send_y), (recv_x, recv_y))
    bonds = ((0, 3), (1, 4))
    quarter = ALPHA_T * 0.5

    def beside(axis, side):
        return here[axis] + (1 if side == 0 else -1)

    def present(axis, side):
        index = beside(axis, side)
        return jnp.logical_and(index >= 0, index < sizes[axis])

    def place(axis, side):
        index = beside(axis, side)
        return (index, here[1]) if axis == 0 else (here[0], index)

    def edge_copy(turn, axis, side):
        return pltpu.make_async_remote_copy(
            src_ref=sends[axis].at[turn, side],
            dst_ref=recvs[axis].at[turn, 1 - side],
            send_sem=send_sem.at[turn, axis, side],
            recv_sem=recv_sem.at[turn, axis, 1 - side],
            device_id=place(axis, side),
            device_id_type=MESH,
        )

    pairs = [(axis, side) for axis in (1, 0) for side in (0, 1)]
    barrier = pltpu.get_barrier_semaphore()
    for axis, side in pairs:

        @pl.when(present(axis, side))
        def _():
            pl.semaphore_signal(barrier, inc=1, device_id=place(axis, side), device_id_type=MESH)

    def fetch(x, y):
        temperature = arrived[source_row[x * columns_y + y]]
        bricks[x, y] = temperature
        value = displacement[x, y].astype(jnp.float32) - quarter * temperature.astype(jnp.float32)
        stretch[x + 1, y] = value
        return value.astype(jnp.bfloat16)

    def launch(turn, axis):
        for side in (0, 1):

            @pl.when(present(axis, side))
            def _():
                edge_copy(turn, axis, side).start()

    def arrive(turn, axis, side, add):
        @pl.when(present(axis, side))
        def _():
            edge_copy(turn, axis, 1 - side).wait_recv()
            if axis == 0:
                for y in range(columns_y):
                    add(columns_x - 1 if side == 0 else 0, y, y)
            else:

                @pl.loop(0, columns_x)
                def _(x):
                    add(x, columns_y - 1 if side == 0 else 0, x)

    def bond_sum(field, x, y):
        middle = field[x + 1, y]
        bond = [live[d, x * columns_y + y].astype(jnp.float32) for d in range(6)]
        result = bond[0] * field[x + 2, y] + bond[3] * field[x, y]
        result = result + bond[2] * pltpu.roll(middle, length - 1, 0)
        result = result + bond[5] * pltpu.roll(middle, 1, 0)
        if y + 1 < columns_y:
            result = result + bond[1] * field[x + 1, y + 1]
        if y > 0:
            result = result + bond[4] * field[x + 1, y - 1]
        count = bond[0] + bond[1] + bond[2] + bond[3] + bond[4] + bond[5]
        return middle, result, count

    @pl.loop(0, columns_x)
    def _(x):
        send_y[0, 0, x] = fetch(x, columns_y - 1)
        send_y[0, 1, x] = fetch(x, 0)

    peers = sum(jnp.where(present(axis, side), 1, 0) for axis, side in pairs)
    pl.semaphore_wait(barrier, peers)
    launch(0, 1)

    @pl.loop(0, columns_x)
    def _(x):
        for y in range(1, columns_y - 1):
            fetch(x, y)

    for y in range(columns_y):
        send_x[0, 0, y] = stretch[columns_x, y].astype(jnp.bfloat16)
        send_x[0, 1, y] = stretch[1, y].astype(jnp.bfloat16)
    launch(0, 0)

    nothing = jnp.zeros((length, cases), jnp.float32)
    for field in (stretch, dilation):
        for y in range(columns_y):
            field[0, y] = nothing
            field[columns_x + 1, y] = nothing

    columns = columns_x * columns_y
    for first in range(0, 6 * columns, length):
        turned = bond_live[first : first + length].astype(jnp.float32).T
        for j in range(turned.shape[1]):
            live[(first + j) // columns, (first + j) % columns] = jnp.broadcast_to(
                turned[:, j : j + 1], (length, cases)
            ).astype(jnp.bfloat16)

    @pl.loop(0, columns_x)
    def _(x):
        for y in range(columns_y):
            _, result, count = bond_sum(stretch, x, y)
            other = displacement[x, y].astype(jnp.float32) + quarter * bricks[x, y].astype(
                jnp.float32
            )
            dilation[x + 1, y] = (result - count * other) * (1.0 / 6.0)

    def complete(axis, side):
        def add(x, y, at):
            bond = live[bonds[axis][side], x * columns_y + y].astype(jnp.float32)
            value = recvs[axis][0, side, at].astype(jnp.float32)
            dilation[x + 1, y] = dilation[x + 1, y] + bond * value * (1.0 / 6.0)

        arrive(0, axis, side, add)

    for axis, side in reversed(pairs):
        complete(axis, side)

    @pl.loop(0, columns_x)
    def _(x):
        send_y[1, 0, x] = dilation[x + 1, columns_y - 1].astype(jnp.bfloat16)
        send_y[1, 1, x] = dilation[x + 1, 0].astype(jnp.bfloat16)

    launch(1, 1)
    for y in range(columns_y):
        send_x[1, 0, y] = dilation[columns_x, y].astype(jnp.bfloat16)
        send_x[1, 1, y] = dilation[1, y].astype(jnp.bfloat16)
    launch(1, 0)

    @pl.loop(0, columns_x)
    def _(x):
        for y in range(columns_y):
            middle, result, count = bond_sum(dilation, x, y)
            force = (6.0 * BOND_STIFFNESS) * middle + STATE_STIFFNESS * (result - count * middle)
            value = displacement[x, y].astype(jnp.float32) + STEP_SIZE * force
            stretch[x + 1, y] = value
            if 0 < y < columns_y - 1:
                moved[x, y] = value.astype(jnp.bfloat16)

    def finish(axis, side):
        def add(x, y, at):
            bond = live[bonds[axis][side], x * columns_y + y].astype(jnp.float32)
            value = recvs[axis][1, side, at].astype(jnp.float32)
            value = stretch[x + 1, y] + (STEP_SIZE * STATE_STIFFNESS) * (bond * value)
            stretch[x + 1, y] = value
            if axis == 0 and 0 < y < columns_y - 1:
                moved[x, y] = value.astype(jnp.bfloat16)

        arrive(1, axis, side, add)

    for axis, side in reversed(pairs):
        finish(axis, side)

    @pl.loop(0, columns_x)
    def _(x):
        for y in (0, columns_y - 1):
            moved[x, y] = stretch[x + 1, y].astype(jnp.bfloat16)

    for turn in (0, 1):
        for axis, side in pairs:

            @pl.when(present(axis, side))
            def _():
                edge_copy(turn, axis, side).wait_send()


def mechanics(source_row, arrived, displacement, bond_live):
    columns_x, columns_y, length, cases = displacement.shape
    columns = columns_x * columns_y
    vmem = pl.BlockSpec(memory_space=pltpu.VMEM)
    field = pltpu.VMEM((columns_x + 2, columns_y, length, cases), jnp.float32)
    edge_x = pltpu.VMEM((2, 2, columns_y, length, cases), jnp.bfloat16)
    edge_y = pltpu.VMEM((2, 2, columns_x, length, cases), jnp.bfloat16)
    out = jax.ShapeDtypeStruct(displacement.shape, jnp.bfloat16)
    return pl.pallas_call(
        mechanics_kernel,
        out_shape=(out, out),
        in_specs=[pl.BlockSpec(memory_space=pltpu.SMEM), vmem, vmem, vmem],
        out_specs=(vmem, vmem),
        scratch_shapes=[
            field,
            field,
            pltpu.VMEM((6, columns, length, cases), jnp.bfloat16),
            edge_x,
            edge_y,
            edge_x,
            edge_y,
            pltpu.SemaphoreType.DMA((2, 2, 2)),
            pltpu.SemaphoreType.DMA((2, 2, 2)),
        ],
        compiler_params=pltpu.CompilerParams(
            collective_id=1, has_side_effects=True, vmem_limit_bytes=50 * MIB
        ),
        name="mechanics",
    )(source_row, arrived, displacement, bond_live.reshape(6 * columns, length))


def local(
    heat_source,
    diagonal,
    active,
    conductance,
    pattern,
    send_list,
    owner_map,
    displacement,
    bond_live,
):
    blocks, tile_count, length = conductance.shape[:3]
    cases = heat_source.shape[1]
    devices = lax.axis_size(("row", "col"))
    me = lax.axis_index(("row", "col"))
    cap = max(1, blocks // devices)

    slots = jnp.arange(blocks, dtype=jnp.int32)
    mine = lax.dynamic_slice_in_dim(owner_map, me * blocks, blocks, axis=1)
    my_distance = (mine[0] - me + devices) % devices
    of_slot = mine[1][None, :] == slots[:, None]
    block_of = jnp.sum(jnp.where(of_slot, slots[None, :], 0), axis=1)
    distance = jnp.sum(jnp.where(of_slot, my_distance[None, :], 0), axis=1)
    rank = jnp.sum(
        ((distance[:, None] == distance[None, :]) & (slots[None, :] < slots[:, None])).astype(
            jnp.int32
        ),
        axis=1,
    )
    target = ((me + distance) % devices) * cap + rank
    places = jnp.arange(devices * cap, dtype=jnp.int32)
    route = jnp.sum(jnp.where(target[None, :] == places[:, None], block_of[None, :], 0), axis=1)
    source_row = ((me - distance + devices) % devices) * cap + rank

    arrived = chebyshev(
        pattern,
        send_list,
        route,
        heat_source.reshape(blocks, length, cases),
        active.reshape(blocks, length),
        diagonal.reshape(blocks, length),
        conductance,
    )
    return mechanics(source_row, arrived, displacement, bond_live)


def solution(mesh):
    return jax.shard_map(
        local,
        mesh=mesh,
        in_specs=(
            P(("row", "col"), None),
            P(("row", "col")),
            P(("row", "col")),
            P(("row", "col"), None, None, None),
            P(("row", "col"), None),
            P(("row", "col"), None, None),
            P(),
            P("row", "col", None, None),
            P(None, "row", "col", None),
        ),
        out_specs=(P("row", "col", None, None), P("row", "col", None, None)),
        check_vma=False,
    )
```
